128 devices in a mesh: seq: 2 (over y_lo), col: 16 (over y_hi, z, core), tp: 4 (over x).
Axes of the slice: x: 4, y: 4 (y_hi: 2, y_lo: 2; y = y_hi * 2 + y_lo), z: 4, core: 2. Of those that a mesh axis runs over, the one named last changes fastest.
Arguments:
- inputs: bfloat16 [4096, 8192], P(('seq', 'tp'), 'col'), may hold values from -6 to 6
- grads: bfloat16 [4096, 8192], P(('seq', 'tp'), 'col'), may hold values from -0.035888672 to 0.035888672
- h_in: bfloat16 [8192, 8192], P(None, 'col'), may hold values from -0.0625 to 0.0625
- segments: int32 [8, 512], P(('seq', 'tp')), may hold values from 0 to 3, never falling along the last dimension, each value on 1 to 256 neighbouring positions
Outputs:
- h_out: float32 [8192, 8192], P(('seq', 'tp'), 'col')
The draws below stay inside these ranges and needn't reach their ends.
Inputs may be any that keep to these rules, and one draw needn't show every extreme that they name: `segments`: within each sequence the numbers never fall; every document has 1 to 256 tokens.
All inputs are finite; a program needn't handle non-finite values.
Results may differ from the reference program's by a relative error of at most 0.005.
Values may be sent and summed in bfloat16 or wider, within the bound.
No kernel may reach another device: no remote copies, remote signals or barrier semaphores. Data moves between devices by JAX's collectives and lax.ppermute only.
A program may use at most 128 MiB of HBM per device.

```python
import math
import jax
import jax.numpy as jnp
import numpy as np

DIN = 8192
DOUT = 8192
SEQ_LEN = 512
SEQS = 8


def level_of(key, shape, cuts, low, largest):
    gain = 1.0
    for position, parts in cuts:
        heights = jax.random.uniform(jax.random.fold_in(jax.random.fold_in(key, 6), position), (parts,), jnp.float32, low / len(cuts), largest / len(cuts))
        gain = gain * jnp.repeat(jnp.exp(heights), shape[position] // parts).reshape((-1,) + (1,) * (len(shape) - 1 - position))
    return gain


def profile(amount, total, most, lean):
    weights = [(1 << 20) // math.isqrt(rank ** lean) + 1 for rank in range(2, amount + 1)]
    rest, given = total - most - (amount - 1), [1] * (amount - 1)
    while rest > 0:
        free = [i for i in range(amount - 1) if given[i] < most]
        pool, remaining = sum([weights[i] for i in free]), rest
        for i in free:
            extra = min(most - given[i], max(1, remaining * weights[i] // pool), rest)
            given[i] = given[i] + extra
            rest = rest - extra
    return np.array([most] + given)


def uneven(own_key, amount, total, most, lean):
    if amount == 2:
        one = jax.random.randint(own_key, (), max(1, total - most), min(most, total - 1) + 1)
        return jnp.stack([one, total - one])
    tallies = jnp.asarray(profile(amount, total, most, lean), jnp.int32)
    pairs = (amount - 1) // 2
    source_of, taker = tallies[1:1 + 2 * pairs:2], tallies[2:2 + 2 * pairs:2]
    room = jnp.minimum(source_of - 1, most - taker)
    shifted = jax.random.randint(jax.random.fold_in(own_key, 1), (pairs,), 0, 1 << 20) % (room + 1)
    tallies = tallies.at[1:1 + 2 * pairs:2].set(source_of - shifted).at[2:2 + 2 * pairs:2].set(taker + shifted)
    return tallies[jax.random.permutation(jax.random.fold_in(own_key, 2), amount)]


def noise(key, dims, deviation, limit, shards=(), dtype=jnp.bfloat16):
    drawn = jax.random.normal(key, dims, jnp.float32) * deviation
    if len(shards) > 0:
        drawn = level_of(key, dims, shards, -0.22, 0.18) * drawn
    return jnp.clip(drawn, min=-limit, max=limit).astype(dtype)


def setup_inputs(seed: int = 0) -> dict:
    keys = jax.random.split(jax.random.key(seed), 5)
    return {
        "inputs": noise(keys[0], (SEQS * SEQ_LEN, DIN), 1.0, 6.0, ((0, 8), (1, 16))),
        "grads": noise(keys[1], (SEQS * SEQ_LEN, DOUT), 0.006, 0.035888672, ((0, 8), (1, 16))),
        "h_in": noise(keys[2], (DIN, DIN), DIN ** -0.5, 0.0625, ((1, 16),)),
        "segments": jax.vmap(lambda own: jnp.searchsorted(jnp.cumsum(uneven(own, 4, SEQ_LEN, SEQ_LEN // 2, 0)), jnp.arange(SEQ_LEN), side="right"))(jax.random.split(keys[3], SEQS)).reshape((SEQS, SEQ_LEN)).astype(jnp.int32),
    }


def reference(inputs, grads, h_in, segments):
    summed = jnp.zeros((DOUT, DOUT), jnp.float32)
    for sequence in range(SEQS):
        lower = sequence * SEQ_LEN
        x_rows = inputs[lower:lower + SEQ_LEN]
        d_rows = grads[lower:lower + SEQ_LEN]
        projected = jnp.dot(x_rows, h_in, preferred_element_type=jnp.float32).astype(jnp.bfloat16)
        square = jnp.dot(projected, x_rows.T, preferred_element_type=jnp.float32)
        labels = segments[sequence]
        same = labels[:, None] == labels[None, :]
        masked = jnp.where(same, square, jnp.float32(0.0)).astype(jnp.bfloat16)
        product = jnp.dot(masked, d_rows, preferred_element_type=jnp.float32).astype(jnp.bfloat16)
        summed = summed + jnp.dot(d_rows.T, product, preferred_element_type=jnp.float32)
    return summed
```

```python
import jax
import jax.numpy as jnp
from jax import lax
from jax.sharding import Mesh, PartitionSpec as P

AXES = ("yl", "yh", "z", "k", "x")
SIZES = (2, 2, 4, 2, 4)
F32 = jnp.float32
BF16 = jnp.bfloat16


def linear(place):
    index = 0
    for part, size in zip(place, SIZES):
        index = index * size + part
    return index


def place_of(index):
    parts = []
    for size in reversed(SIZES):
        parts.append(index % size)
        index //= size
    return tuple(reversed(parts))


def move(value, where):
    pairs = [(i, linear(where(*place_of(i)))) for i in range(128)]
    return lax.ppermute(value, AXES, pairs)


def z_up(yl, yh, z, k, x):
    return yl, yh, (z + 1) % 4, k, x


def z_down(yl, yh, z, k, x):
    return yl, yh, (z - 1) % 4, k, x


def x_up(yl, yh, z, k, x):
    return yl, yh, z, k, (x + 1) % 4


def x_down(yl, yh, z, k, x):
    return yl, yh, z, k, (x - 1) % 4


def swap_yh(yl, yh, z, k, x):
    return yl, 1 - yh, z, k, x


def swap_yl(yl, yh, z, k, x):
    return 1 - yl, yh, z, k, x


def swap_core(yl, yh, z, k, x):
    return yl, yh, z, 1 - k, x


def z_pair_a(yl, yh, z, k, x):
    return yl, yh, z ^ 1, k, x


def z_pair_b(yl, yh, z, k, x):
    return yl, yh, (z + 1 if z % 2 else z - 1) % 4, k, x


def shear(yl, yh, z, k, x):
    return yl, yh, (z + x) % 4, k, x


def reflect(yl, yh, z, k, x):
    return yh, yl, z, k, (z - x) % 4


def gather8(own, cut, up, down, across):
    below = move(own, up)
    above = move(own, down)
    over = move(own, across)
    top = move(below[:cut], up)
    bottom = move(above[cut:], down)
    over_below = move(over, up)
    over_above = move(over, down)
    over_top = move(top, across)
    over_bottom = move(bottom, across)
    far = jnp.concatenate([top, bottom])
    over_far = jnp.concatenate([over_top, over_bottom])
    return [own, above, far, below, over, over_above, over_far, over_below]


def per_device(inputs, grads, h_in, segments):
    yl, yh, z, k, x = (lax.axis_index(name) for name in AXES)

    xs = gather8(inputs, 256, z_up, z_down, swap_yh)
    order = [(yh ^ a) * 4 + (z + b) % 4 for a in range(2) for b in range(4)]
    h_mine = jnp.concatenate(
        [lax.dynamic_slice(h_in, (i * 1024 + k * 512, 0), (512, 512)) for i in order]
    )
    h_send = jnp.concatenate(
        [lax.dynamic_slice(h_in, (i * 1024 + (1 - k) * 512, 0), (512, 512)) for i in order]
    )
    h_core = move(h_send, swap_core)
    x_half = jnp.concatenate(xs, axis=1)
    y_mine = jnp.dot(x_half, h_mine, preferred_element_type=F32)
    y_send = jnp.dot(x_half, h_core, preferred_element_type=F32)
    y = (y_mine + move(y_send, swap_core)).astype(BF16)
    p = lax.dot_general(y, inputs, (((1,), (1,)), ((), ())), preferred_element_type=F32)
    seg = segments[0]
    same = seg[:, None] == seg[None, :]
    folded = jnp.where(same[:, :256], p[:, :256], jnp.where(same[:, 256:], p[:, 256:], 0.0))
    acc = lax.dynamic_slice(folded, (k * 256, 0), (256, 256)) + move(
        lax.dynamic_slice(folded, ((1 - k) * 256, 0), (256, 256)), swap_core
    )
    for where in (swap_yh, z_pair_a, z_pair_b):
        acc = acc + move(acc.astype(BF16), where).astype(F32)
    kh = acc.astype(BF16)
    pair = jnp.stack([kh, move(kh, swap_yl)])
    below = move(pair, x_up)
    above = move(pair, x_down)
    far = jnp.stack([move(below[0], x_up), move(above[1], x_down)])
    halves = jnp.stack([pair[0], above[0], far[0], below[0], pair[1], above[1], far[1], below[1]])
    other = move(halves, swap_core)
    first = jnp.where(k == 0, halves, other)
    second = jnp.where(k == 0, other, halves)
    k_all = jnp.concatenate([first, second], axis=1)

    marked = jnp.concatenate([grads, jnp.broadcast_to(segments.astype(BF16), (16, 512))])
    ds = jnp.stack(gather8(marked, 256, x_up, x_down, swap_yl))
    d_c = ds[:, :512]
    seg_all = ds[:, 512]
    same_all = seg_all[:, :, None] == seg_all[:, None, :]
    k_full = jnp.concatenate(
        [
            jnp.where(same_all[:, :, :256], k_all, jnp.zeros((), BF16)),
            jnp.where(same_all[:, :, 256:], k_all, jnp.zeros((), BF16)),
        ],
        axis=2,
    )
    z_all = lax.dot_general(
        k_full, d_c, (((2,), (1,)), ((0,), (0,))), preferred_element_type=F32
    ).astype(BF16)

    turned = move(move(grads, shear), reflect)
    rs = gather8(turned, 256, z_up, z_down, swap_yh)
    r_mine = jnp.stack(rs)
    r_core = move(r_mine, swap_core)
    pick = jnp.stack(
        [(yl ^ a ^ yh) * 4 + (2 * x + b - z) % 4 for a in range(2) for b in range(4)]
    )
    r_mine = jnp.take(r_mine, pick, axis=0).reshape(4096, 512)
    r_core = jnp.take(r_core, pick, axis=0).reshape(4096, 512)
    z_flat = z_all.reshape(4096, 512)
    out_mine = lax.dot_general(r_mine, z_flat, (((0,), (0,)), ((), ())), preferred_element_type=F32)
    out_core = lax.dot_general(r_core, z_flat, (((0,), (0,)), ((), ())), preferred_element_type=F32)
    return jnp.concatenate(
        [jnp.where(k == 0, out_mine, out_core), jnp.where(k == 0, out_core, out_mine)]
    )


def solution(mesh):
    fine = Mesh(mesh.devices.reshape(SIZES), AXES)
    col = ("yh", "z", "k")
    row = ("yl", "x")
    return jax.shard_map(
        per_device,
        mesh=fine,
        in_specs=(P(row, col), P(row, col), P(None, col), P(row, None)),
        out_specs=P(row, col),
        check_vma=False,
    )
```

```python
import functools

import jax
import jax.numpy as jnp
from jax import lax
from jax.experimental import pallas as pl
from jax.experimental.pallas import tpu as pltpu
from jax.sharding import Mesh, PartitionSpec as P

AXES = ("yl", "yh", "z", "k", "x")
SIZES = (2, 2, 4, 2, 4)

F32 = jnp.float32
BF16 = jnp.bfloat16


def linear(place):
    index = 0
    for part, size in zip(place, SIZES):
        index = index * size + part
    return index


def place_of(index):
    parts = []
    for size in reversed(SIZES):
        parts.append(index % size)
        index //= size
    return tuple(reversed(parts))


def move(value, where):
    pairs = [(i, linear(where(*place_of(i)))) for i in range(128)]
    return lax.ppermute(value, AXES, pairs)


def z_up(yl, yh, z, k, x):
    return yl, yh, (z + 1) % 4, k, x


def z_down(yl, yh, z, k, x):
    return yl, yh, (z - 1) % 4, k, x


def x_up(yl, yh, z, k, x):
    return yl, yh, z, k, (x + 1) % 4


def x_down(yl, yh, z, k, x):
    return yl, yh, z, k, (x - 1) % 4


def swap_yh(yl, yh, z, k, x):
    return yl, 1 - yh, z, k, x


def swap_yl(yl, yh, z, k, x):
    return 1 - yl, yh, z, k, x


def swap_core(yl, yh, z, k, x):
    return yl, yh, z, 1 - k, x


def z_pair_a(yl, yh, z, k, x):
    return yl, yh, z ^ 1, k, x


def z_pair_b(yl, yh, z, k, x):
    return yl, yh, (z + 1 if z % 2 else z - 1) % 4, k, x


def shear(yl, yh, z, k, x):
    return yl, yh, (z + x) % 4, k, x


def reflect(yl, yh, z, k, x):
    return yh, yl, z, k, (z - x) % 4


def gather8(own, cut, up, down, across):
    below = move(own, up)
    above = move(own, down)
    over = move(own, across)
    top = move(below[:cut], up)
    bottom = move(above[cut:], down)
    over_below = move(over, up)
    over_above = move(over, down)
    over_top = move(top, across)
    over_bottom = move(bottom, across)
    far = jnp.concatenate([top, bottom])
    over_far = jnp.concatenate([over_top, over_bottom])
    return [own, above, far, below, over, over_above, over_far, over_below]


def gather7(own, up, down, across):
    below = move(own, up)
    above = move(own, down)
    over = move(own, across)
    far = move(below, up)
    over_below = move(over, up)
    over_above = move(over, down)
    over_far = move(over_above, down)
    return [own, above, far, below, over, over_above, over_far, over_below]


VMEM = pl.BlockSpec(memory_space=pltpu.VMEM)
ANY = pl.BlockSpec(memory_space=pl.ANY)
SMEM = pl.BlockSpec(memory_space=pltpu.SMEM)
MIB = 1 << 20


def y_body(n, first, where, *refs):
    xs, refs = refs[:n], refs[n:]
    h, h_core, refs = refs[0], refs[1], refs[2:]
    if first:
        before = (None, None)
    else:
        before, refs = refs[:2], refs[2:]
    out_mine, out_send, held, sem = refs

    def copies(j):
        row = pl.multiple_of(where[j], 512)
        return (
            pltpu.make_async_copy(h.at[pl.ds(row, 512), :], held.at[j, 0], sem.at[j, 0]),
            pltpu.make_async_copy(h_core.at[where[n + j]], held.at[j, 1], sem.at[j, 1]),
        )

    for j in range(n):
        for copy in copies(j):
            copy.start()
    for j in range(n):
        for copy in copies(j):
            copy.wait()
        for i, (old, new) in enumerate(zip(before, (out_mine, out_send))):
            term = jnp.dot(xs[j][...], held[j, i], preferred_element_type=F32)
            if j > 0:
                new[...] += term
            elif first:
                new[...] = term
            else:
                new[...] = old[...] + term


def y_stage(xs, where, h, h_core, before):
    n = len(xs)
    first = before is None
    before = () if first else before
    return pl.pallas_call(
        functools.partial(y_body, n, first),
        out_shape=[jax.ShapeDtypeStruct((512, 512), F32)] * 2,
        in_specs=[SMEM] + [VMEM] * n + [ANY, ANY] + [VMEM] * len(before),
        out_specs=[VMEM, VMEM],
        scratch_shapes=[
            pltpu.VMEM((n, 2, 512, 512), BF16),
            pltpu.SemaphoreType.DMA((n, 2)),
        ],
        compiler_params=pltpu.CompilerParams(vmem_limit_bytes=24 * MIB),
        cost_estimate=pl.CostEstimate(
            flops=n * (1 << 29), bytes_accessed=n * MIB + 4 * MIB, transcendentals=0
        ),
        name="y_stage",
    )(where, *xs, h, h_core, *before)


def p_body(core, y_mine, y_got, x, lower, upper, out_mine, out_send, held):
    y = (y_mine[...] + y_got[...]).astype(BF16)
    p = lax.dot_general(y, x[...], (((1,), (1,)), ((), ())), preferred_element_type=F32)
    held[...] = jnp.where(lower[...] > 0, p[:, :256], jnp.where(upper[...] > 0, p[:, 256:], 0.0))
    k = core[0]
    out_mine[...] = held[pl.ds(pl.multiple_of(k * 256, 256), 256), :]
    out_send[...] = held[pl.ds(pl.multiple_of((1 - k) * 256, 256), 256), :]


def p_stage(core, y_mine, y_got, x, lower, upper):
    return pl.pallas_call(
        p_body,
        out_shape=[jax.ShapeDtypeStruct((256, 256), F32)] * 2,
        in_specs=[SMEM] + [VMEM] * 5,
        out_specs=[VMEM, VMEM],
        scratch_shapes=[pltpu.VMEM((512, 256), F32)],
        compiler_params=pltpu.CompilerParams(vmem_limit_bytes=16 * MIB),
        cost_estimate=pl.CostEstimate(flops=1 << 28, bytes_accessed=4 * MIB, transcendentals=0),
        name="p_stage",
    )(core, y_mine, y_got, x, lower, upper)


def out_body(n, first, core, *refs):
    k_mine, k_other, refs = refs[0], refs[1], refs[2:]
    lowers, refs = refs[:n], refs[n:]
    ds, refs = refs[:n], refs[n:]
    r_mine, r_core, refs = refs[:8], refs[8:16], refs[16:]
    if not first:
        before, refs = refs[0], refs[1:]
    out, held, z, sem = refs
    k = core[0]
    for i in range(n):
        for j in range(8):

            @pl.when(core[1 + i] == j)
            def _():
                pltpu.make_async_copy(r_mine[j], held.at[i, 0], sem.at[i, 0]).start()
                pltpu.make_async_copy(r_core[j], held.at[i, 1], sem.at[i, 1]).start()

    for i in range(n):
        for part, where in ((k_mine, k), (k_other, 1 - k)):
            rows = pl.ds(pl.multiple_of(where * 256, 256), 256)
            whole = part[i]
            low = whole * lowers[i][rows, :]
            high = whole - low
            z[rows, :] = (
                jnp.dot(low, ds[i][:256], preferred_element_type=F32)
                + jnp.dot(high, ds[i][256:512], preferred_element_type=F32)
            ).astype(BF16)
        for side, where in ((0, k), (1, 1 - k)):
            pltpu.make_async_copy(r_mine[0], held.at[i, side], sem.at[i, side]).wait()
            rows = pl.ds(pl.multiple_of(where * 512, 512), 512)
            term = lax.dot_general(
                held[i, side], z[...], (((0,), (0,)), ((), ())), preferred_element_type=F32
            )
            if i > 0:
                out[rows, :] += term
            elif first:
                out[rows, :] = term
            else:
                out[rows, :] = before[rows, :] + term


def out_stage(core, k_mine, k_other, lowers, ds, r_mine, r_core, before):
    n = len(ds)
    before = () if before is None else (before,)
    return pl.pallas_call(
        functools.partial(out_body, n, not before),
        out_shape=jax.ShapeDtypeStruct((1024, 512), F32),
        in_specs=[SMEM] + [VMEM] * (2 + 2 * n) + [ANY] * 16 + [VMEM] * len(before),
        out_specs=VMEM,
        scratch_shapes=[
            pltpu.VMEM((n, 2, 512, 512), BF16),
            pltpu.VMEM((512, 512), BF16),
            pltpu.SemaphoreType.DMA((n, 2)),
        ],
        compiler_params=pltpu.CompilerParams(vmem_limit_bytes=24 * MIB),
        cost_estimate=pl.CostEstimate(
            flops=n * 6 * (1 << 27), bytes_accessed=n * 2 * MIB + 4 * MIB, transcendentals=0
        ),
        name="out_stage",
    )(core, k_mine, k_other, *lowers, *ds, *r_mine, *r_core, *before)


def per_device(inputs, grads, h_in, segments):
    yl, yh, z, k, x = (lax.axis_index(name) for name in AXES)
    core = jnp.stack([k])

    xs = gather8(inputs, 256, z_up, z_down, swap_yh)
    h_send = lax.dynamic_slice(
        h_in.reshape(8, 2, 512, 512), (0, 1 - k, 0, 0), (8, 1, 512, 512)
    ).reshape(8, 512, 512)
    h_core = move(h_send, swap_core)
    order = [(yh ^ a) * 4 + (z + b) % 4 for a in range(2) for b in range(4)]

    def places(chosen):
        return jnp.stack([order[i] * 1024 + k * 512 for i in chosen] + [order[i] for i in chosen])

    sums = None
    for chosen in ((0, 1, 3, 4), (2, 5, 7), (6,)):
        sums = y_stage([xs[i] for i in chosen], places(chosen), h_in, h_core, sums)
    y_mine, y_send = sums
    seg = segments[0]
    same = (seg[:, None] == seg[None, :]).astype(BF16)
    p_mine, p_send = p_stage(
        core, y_mine, move(y_send, swap_core), inputs, same[:, :256], same[:, 256:]
    )
    acc = p_mine + move(p_send, swap_core)
    for where in (swap_yh, z_pair_a, z_pair_b):
        acc = acc + move(acc.astype(BF16), where).astype(F32)
    kh = acc.astype(BF16)
    pair = jnp.stack([kh, move(kh, swap_yl)])
    below = move(pair, x_up)
    above = move(pair, x_down)
    far = jnp.stack([move(below[0], x_up), move(above[1], x_down)])
    near = jnp.concatenate([above, below])

    marked = jnp.concatenate([grads, jnp.broadcast_to(segments.astype(BF16), (16, 512))])
    ds = gather7(marked, x_up, x_down, swap_yl)
    lowers = [(d[512, :, None] == d[512, None, :256]).astype(BF16) for d in ds]
    turned = move(move(grads, shear), reflect)
    r_mine = gather7(turned, z_up, z_down, swap_yh)
    r_core = [move(r, swap_core) for r in r_mine]

    out = None
    for chosen, part in (((0, 4), pair), ((1, 5, 3, 7), near), ((2, 6), far)):
        pick = [(yl ^ (i // 4) ^ yh) * 4 + (2 * x + i % 4 - z) % 4 for i in chosen]
        out = out_stage(
            jnp.stack([k] + pick),
            part,
            move(part, swap_core),
            [lowers[i] for i in chosen],
            [ds[i] for i in chosen],
            r_mine,
            r_core,
            out,
        )
    return out


def solution(mesh):
    fine = Mesh(mesh.devices.reshape(SIZES), AXES)
    col = ("yh", "z", "k")
    row = ("yl", "x")
    return jax.shard_map(
        per_device,
        mesh=fine,
        in_specs=(P(row, col), P(row, col), P(None, col), P(row, None)),
        out_specs=P(row, col),
        check_vma=False,
    )
```

```python
import functools

import jax
import jax.numpy as jnp
from jax import lax
from jax.experimental import pallas as pl
from jax.experimental.pallas import tpu as pltpu
from jax.sharding import Mesh, PartitionSpec as P


AXES = ("yl", "yh", "z", "k", "x")
SIZES = (2, 2, 4, 2, 4)

F32 = jnp.float32
BF16 = jnp.bfloat16


def linear(place):
    index = 0
    for part, size in zip(place, SIZES):
        index = index * size + part
    return index


def place_of(index):
    parts = []
    for size in reversed(SIZES):
        parts.append(index % size)
        index //= size
    return tuple(reversed(parts))


def move(value, where):
    pairs = [(i, linear(where(*place_of(i)))) for i in range(128)]
    return lax.ppermute(value, AXES, pairs)


def z_up(yl, yh, z, k, x):
    return yl, yh, (z + 1) % 4, k, x


def z_down(yl, yh, z, k, x):
    return yl, yh, (z - 1) % 4, k, x


def x_up(yl, yh, z, k, x):
    return yl, yh, z, k, (x + 1) % 4


def x_down(yl, yh, z, k, x):
    return yl, yh, z, k, (x - 1) % 4


def swap_yh(yl, yh, z, k, x):
    return yl, 1 - yh, z, k, x


def swap_yl(yl, yh, z, k, x):
    return 1 - yl, yh, z, k, x


def swap_core(yl, yh, z, k, x):
    return yl, yh, z, 1 - k, x


def z_pair_a(yl, yh, z, k, x):
    return yl, yh, z ^ 1, k, x


def z_pair_b(yl, yh, z, k, x):
    return yl, yh, (z + 1 if z % 2 else z - 1) % 4, k, x


def shear(yl, yh, z, k, x):
    return yl, yh, (z + x) % 4, k, x


def reflect(yl, yh, z, k, x):
    return yh, yl, z, k, (z - x) % 4


def z_far(yl, yh, z, k, x):
    return yl, yh, (z + 2) % 4, k, x


def x_far(yl, yh, z, k, x):
    return yl, yh, z, k, (x + 2) % 4


def gather(own, up, down, two, across, cut):
    below = move(own, up)
    above = move(own, down)
    over = move(own, across)
    over_below = move(over, up)
    over_above = move(over, down)
    if cut is None:
        far = (move(own, two),)
        over_far = (move(far[0], across),)
    else:
        far = (move(below[:cut], up), move(above[cut:], down))
        over_far = (move(far[0], across), move(far[1], across))
    return [own, above, far, below, over, over_above, over_far, over_below]


VMEM = pl.BlockSpec(memory_space=pltpu.VMEM)
HBM = pl.BlockSpec(memory_space=pltpu.HBM)
ANY = pl.BlockSpec(memory_space=pl.ANY)
SMEM = pl.BlockSpec(memory_space=pltpu.SMEM)
MIB = 1 << 20


def cut_body(core, mine, other, out):
    rows = pl.ds(pl.multiple_of(core[0] * 256, 256), 256)
    out[:, :512] = mine[rows, :]
    out[:, 512:] = other[rows, :]


def cut_rows(core, mine, other):
    return pl.pallas_call(
        cut_body,
        out_shape=jax.ShapeDtypeStruct((256, 1024), BF16),
        in_specs=[SMEM, VMEM, VMEM],
        out_specs=VMEM,
        compiler_params=pltpu.CompilerParams(vmem_limit_bytes=4 * MIB),
        cost_estimate=pl.CostEstimate(flops=0, bytes_accessed=MIB, transcendentals=0),
        name="cut_rows",
    )(core, mine, other)


def documents(marked, held):
    columns = jnp.transpose(marked[512:528, :].astype(F32))
    held[...] = jnp.broadcast_to(columns[:, :1], (512, 128))
    return marked[512:513, :].astype(F32)


def y_body(parts, first, last, where, *refs):
    n = len(parts)
    xs = []
    for count in parts:
        xs.append(refs[:count])
        refs = refs[count:]
    h, h_core, refs = refs[0], refs[1], refs[2:]
    if first:
        before = (None, None)
    else:
        before, refs = refs[:2], refs[2:]
    if last:
        x_mine, x_core, marked, folded, sum_mine, sum_core, column, held, sem = refs
        sums = (sum_mine, sum_core)
    else:
        sums, (held, sem) = refs[:2], refs[2:]
    k = where[n]

    def copies(j):
        for t, source in enumerate((h, h_core)):
            for i, part in enumerate((k, 1 - k)):
                row = pl.multiple_of(where[j] * 1024 + part * 512, 512)
                yield pltpu.make_async_copy(
                    source.at[pl.ds(row, 512), :],
                    held.at[j, t, pl.ds(i * 512, 512), :],
                    sem.at[j, t, i],
                )

    for j in range(n):
        for copy in copies(j):
            copy.start()
    for j in range(n):
        for copy in copies(j):
            copy.wait()
        at = 0
        for x in xs[j]:
            rows = slice(at, at + x.shape[0])
            at += x.shape[0]
            for t, (old, new) in enumerate(zip(before, sums)):
                term = jnp.dot(x[...], held[j, t], preferred_element_type=F32)
                if j > 0:
                    new[rows] += term
                elif first:
                    new[rows] = term
                else:
                    new[rows] = old[rows] + term
    if last:
        p = sum(
            lax.dot_general(
                y[...].astype(BF16), x[...], (((1,), (1,)), ((), ())), preferred_element_type=F32
            )
            for y, x in zip(sums, (x_mine, x_core))
        )
        row = documents(marked, column)
        tokens = column[pl.ds(pl.multiple_of(k * 256, 256), 256), :][:, :1]
        folded[...] = jnp.where(
            tokens == row[:, :256], p[:, :256], jnp.where(tokens == row[:, 256:], p[:, 256:], 0.0)
        )


def y_stage(xs, where, h, h_core, before, final=None):
    n = len(xs)
    first = before is None
    before = () if first else before
    xs = [x if isinstance(x, tuple) else (x,) for x in xs]
    parts = tuple(len(x) for x in xs)
    xs = [piece for x in xs for piece in x]
    last = final is not None
    if last:
        out_shape = [jax.ShapeDtypeStruct((256, 256), F32)]
        more = [pltpu.VMEM((256, 512), F32)] * 2 + [pltpu.VMEM((512, 128), F32)]
    else:
        out_shape = [jax.ShapeDtypeStruct((256, 512), F32)] * 2
        more = []
    final = final if last else ()
    return pl.pallas_call(
        functools.partial(y_body, parts, first, last),
        out_shape=out_shape,
        in_specs=[SMEM] + [VMEM] * len(xs) + [HBM, HBM] + [VMEM] * (len(before) + len(final)),
        out_specs=[VMEM] * len(out_shape),
        scratch_shapes=more
        + [pltpu.VMEM((n, 2, 1024, 512), BF16), pltpu.SemaphoreType.DMA((n, 2, 2))],
        compiler_params=pltpu.CompilerParams(vmem_limit_bytes=24 * MIB),
        cost_estimate=pl.CostEstimate(
            flops=n * (1 << 29), bytes_accessed=n * 2 * MIB + 2 * MIB, transcendentals=0
        ),
        name="y_stage",
    )(where, *xs, h, h_core, *before, *final)


def z_body(ks, core, *refs):
    parts, refs = refs[: len(ks)], refs[len(ks) :]
    n = sum(ks)
    mine, other, (out, column) = refs[:n], refs[n : 2 * n], refs[2 * n :]
    rows = pl.ds(pl.multiple_of(core[0] * 256, 256), 256)
    blocks = [part[i, ...] for part, count in zip(parts, ks) for i in range(count)]
    for i in range(n):
        row = documents(mine[i], column)
        low = jnp.where(column[rows, :][:, :1] == row[:, :256], blocks[i], jnp.zeros((), BF16))
        high = blocks[i] - low
        for t, d in enumerate((mine[i], other[i])):
            out[i, :, t * 512 : (t + 1) * 512] = (
                jnp.dot(low, d[:256], preferred_element_type=F32)
                + jnp.dot(high, d[256:512], preferred_element_type=F32)
            ).astype(BF16)


def z_stage(core, parts, mine, other):
    n = len(mine)
    return pl.pallas_call(
        functools.partial(z_body, tuple(part.shape[0] for part in parts)),
        out_shape=jax.ShapeDtypeStruct((n, 256, 1024), BF16),
        in_specs=[SMEM] + [VMEM] * (len(parts) + 2 * n),
        out_specs=VMEM,
        scratch_shapes=[pltpu.VMEM((512, 128), F32)],
        compiler_params=pltpu.CompilerParams(vmem_limit_bytes=24 * MIB),
        cost_estimate=pl.CostEstimate(
            flops=n * (1 << 28), bytes_accessed=n * 2 * MIB, transcendentals=0
        ),
        name="z_stage",
    )(core, *parts, *mine, *other)


def out_body(counts, sides, first, core, *refs):
    n = len(counts)
    rs = []
    for count in counts:
        rs.append(refs[:count])
        refs = refs[count:]
    near, far, refs = refs[0], refs[1], refs[2:]
    if not first:
        before, refs = refs[: len(sides)], refs[len(sides) :]
    outs, (held, z, sem) = refs[: len(sides)], refs[len(sides) :]
    k = core[0]
    width = 512 * len(sides)
    columns = pl.ds(sides[0] * 512, width)
    for i in range(n):
        at = i * 256
        for piece in rs[i]:
            rows = pl.ds(at, piece.shape[0])
            at += piece.shape[0]
            pltpu.make_async_copy(piece, held.at[rows], sem.at[i, 0]).start()
        place = core[1 + i]

        @pl.when(place < 2)
        def _():
            source = near.at[place, :, columns]
            pltpu.make_async_copy(source, z.at[pl.ds(i * 256, 256)], sem.at[i, 1]).start()

        @pl.when(place >= 2)
        def _():
            source = far.at[place - 2, :, columns]
            pltpu.make_async_copy(source, z.at[pl.ds(i * 256, 256)], sem.at[i, 1]).start()

    for i in range(n):
        rows = pl.ds(i * 256, 256)
        pltpu.make_async_copy(held.at[rows], held.at[rows], sem.at[i, 0]).wait()
        pltpu.make_async_copy(z.at[rows], z.at[rows], sem.at[i, 1]).wait()
    for i, part in enumerate((k, 1 - k)):
        rows = pl.ds(pl.multiple_of(part * 512, 512), 512)
        for t in range(len(sides)):
            term = lax.dot_general(
                held[:, i * 512 : (i + 1) * 512],
                z[:, t * 512 : (t + 1) * 512],
                (((0,), (0,)), ((), ())),
                preferred_element_type=F32,
            )
            outs[t][rows, :] = term if first else before[t][rows, :] + term


def out_stage(core, rs, near, far, sides, before):
    n = len(rs)
    counts = tuple(len(r) for r in rs)
    rs = [piece for r in rs for piece in r]
    return pl.pallas_call(
        functools.partial(out_body, counts, sides, not before),
        out_shape=[jax.ShapeDtypeStruct((1024, 512), F32)] * len(sides),
        in_specs=[SMEM] + [ANY] * (len(rs) + 2) + [VMEM] * len(before),
        out_specs=[VMEM] * len(sides),
        scratch_shapes=[
            pltpu.VMEM((n * 256, 1024), BF16),
            pltpu.VMEM((n * 256, 512 * len(sides)), BF16),
            pltpu.SemaphoreType.DMA((n, 2)),
        ],
        compiler_params=pltpu.CompilerParams(vmem_limit_bytes=24 * MIB),
        cost_estimate=pl.CostEstimate(
            flops=n * len(sides) * (1 << 28), bytes_accessed=n * MIB + 4 * MIB, transcendentals=0
        ),
        name="out_stage",
    )(core, *rs, near, far, *before)


EARLY = (0, 1, 3, 4)


def step(inputs, grads, h_in, segments):
    yl, yh, z, k, x = (lax.axis_index(name) for name in AXES)
    core = jnp.stack([k])

    x_core = move(inputs, swap_core)
    x_rows = cut_rows(core, inputs, x_core)
    xs = gather(x_rows, z_up, z_down, z_far, swap_yh, 128)
    h_core = move(h_in, swap_core)
    order = [(yh ^ a) * 4 + (z + b) % 4 for a in range(2) for b in range(4)]
    marked = jnp.concatenate([grads, jnp.broadcast_to(segments.astype(BF16), (16, 512))])

    sums = None
    for turn, chosen in enumerate(((0, 1, 3, 4), (2, 5, 7), (6,))):
        final = (inputs, x_core, marked) if turn == 2 else None
        where = jnp.stack([order[i] for i in chosen] + [k])
        sums = y_stage([xs[i] for i in chosen], where, h_in, h_core, sums, final)
    acc = sums[0]
    for where in (z_pair_a, z_pair_b, swap_yh):
        acc = acc + move(acc.astype(BF16), where).astype(F32)
    kh = acc.astype(BF16)
    pair = jnp.stack([kh, move(kh, swap_yl)])
    below = move(pair, x_up)
    above = move(pair, x_down)
    far = move(pair, x_far)

    ds = gather(marked, x_up, x_down, x_far, swap_yl, None)
    ds = [d[0] if isinstance(d, tuple) else d for d in ds]
    d_core = move(grads, swap_core)
    others = [d_core] + [move(ds[i], swap_core) for i in range(1, 8)]
    z_near = z_stage(core, (pair,), ds[::4], others[::4])
    chosen = (1, 5, 2, 6, 3, 7)
    z_rest = z_stage(
        core, (above, far, below), [ds[i] for i in chosen], [others[i] for i in chosen]
    )

    d_rows = cut_rows(core, grads, d_core)
    turned = move(move(d_rows, shear), reflect)
    rs = gather(turned, z_up, z_down, z_far, swap_yh, 128)
    rs = [r if isinstance(r, tuple) else (r,) for r in rs]
    places = [(z + i % 4 - 2 * x) % 4 * 2 + (yl ^ yh ^ (i // 4)) for i in range(8)]

    early, late = EARLY, [i for i in range(8) if i not in EARLY]
    pick = [jnp.stack([k] + [places[i] for i in some]) for some in (early, late)]
    blocks = [[rs[i] for i in some] for some in (early, late)]
    out_mine, out_send = out_stage(pick[0], blocks[0], z_near, z_rest, (0, 1), ())
    (out_send,) = out_stage(pick[1], blocks[1], z_near, z_rest, (1,), (out_send,))
    out_got = move(out_send, swap_core)
    (out_mine,) = out_stage(pick[1], blocks[1], z_near, z_rest, (0,), (out_mine,))
    return out_mine + out_got


def solution(mesh):
    fine = Mesh(mesh.devices.reshape(SIZES), AXES)
    col = ("yh", "z", "k")
    row = ("yl", "x")
    return jax.shard_map(
        step,
        mesh=fine,
        in_specs=(P(row, col), P(row, col), P(None, col), P(row, None)),
        out_specs=P(row, col),
        check_vma=False,
    )
```

```python
import functools

import jax
import jax.numpy as jnp
from jax import lax
from jax.experimental import pallas as pl
from jax.experimental.pallas import tpu as pltpu
from jax.sharding import Mesh, PartitionSpec as P


AXES = ("yl", "yh", "z", "k", "x")
SIZES = (2, 2, 4, 2, 4)

F32 = jnp.float32
BF16 = jnp.bfloat16


def linear(place):
    index = 0
    for part, size in zip(place, SIZES):
        index = index * size + part
    return index


def place_of(index):
    parts = []
    for size in reversed(SIZES):
        parts.append(index % size)
        index //= size
    return tuple(reversed(parts))


def move(value, where):
    pairs = [(i, linear(where(*place_of(i)))) for i in range(128)]
    return lax.ppermute(value, AXES, pairs)


def z_up(yl, yh, z, k, x):
    return yl, yh, (z + 1) % 4, k, x


def z_down(yl, yh, z, k, x):
    return yl, yh, (z - 1) % 4, k, x


def x_up(yl, yh, z, k, x):
    return yl, yh, z, k, (x + 1) % 4


def x_down(yl, yh, z, k, x):
    return yl, yh, z, k, (x - 1) % 4


def swap_yh(yl, yh, z, k, x):
    return yl, 1 - yh, z, k, x


def swap_yl(yl, yh, z, k, x):
    return 1 - yl, yh, z, k, x


def swap_core(yl, yh, z, k, x):
    return yl, yh, z, 1 - k, x


def z_pair_a(yl, yh, z, k, x):
    return yl, yh, z ^ 1, k, x


def z_pair_b(yl, yh, z, k, x):
    return yl, yh, (z + 1 if z % 2 else z - 1) % 4, k, x


def shear(yl, yh, z, k, x):
    return yl, yh, (z + x + 2 * k) % 4, k, x


def reflect(yl, yh, z, k, x):
    return yh, yl, z, k, (z - x - 2 * k) % 4


def z_far(yl, yh, z, k, x):
    return yl, yh, (z + 2) % 4, k, x


def x_far(yl, yh, z, k, x):
    return yl, yh, z, k, (x + 2) % 4


def gather(own, up, down, two, across, cut):
    below = move(own, up)
    above = move(own, down)
    over = move(own, across)
    over_below = move(over, up)
    over_above = move(over, down)
    if cut is None:
        far = (move(own, two),)
        over_far = (move(far[0], across),)
    else:
        far = (move(below[:cut], up), move(above[cut:], down))
        over_far = (move(far[0], across), move(far[1], across))
    return [own, above, far, below, over, over_above, over_far, over_below]


VMEM = pl.BlockSpec(memory_space=pltpu.VMEM)
HBM = pl.BlockSpec(memory_space=pltpu.HBM)
ANY = pl.BlockSpec(memory_space=pl.ANY)
SMEM = pl.BlockSpec(memory_space=pltpu.SMEM)
MIB = 1 << 20


def cut_body(core, mine, other, out):
    rows = pl.ds(pl.multiple_of(core[0] * 256, 256), 256)
    out[:, :512] = mine[rows, :]
    out[:, 512:] = other[rows, :]


def cut_rows(core, mine, other):
    return pl.pallas_call(
        cut_body,
        out_shape=jax.ShapeDtypeStruct((256, 1024), BF16),
        in_specs=[SMEM, VMEM, VMEM],
        out_specs=VMEM,
        compiler_params=pltpu.CompilerParams(vmem_limit_bytes=4 * MIB),
        cost_estimate=pl.CostEstimate(flops=0, bytes_accessed=MIB, transcendentals=0),
        name="cut_rows",
    )(core, mine, other)


def documents(marked, held):
    columns = jnp.transpose(marked[512:528, :].astype(F32))
    held[...] = jnp.broadcast_to(columns[:, :1], (512, 128))
    return marked[512:513, :].astype(F32)


def y_body(parts, first, last, where, *refs):
    n = len(parts)
    xs = []
    for count in parts:
        xs.append(refs[:count])
        refs = refs[count:]
    h, h_core, refs = refs[0], refs[1], refs[2:]
    if first:
        before = (None, None)
    else:
        before, refs = refs[:2], refs[2:]
    if last:
        x_mine, x_core, marked, folded, sum_mine, sum_core, column, held, sem = refs
        sums = (sum_mine, sum_core)
    else:
        sums, (held, sem) = refs[:2], refs[2:]
    k = where[n]

    def copies(j):
        for t, source in enumerate((h, h_core)):
            for i, part in enumerate((k, 1 - k)):
                row = pl.multiple_of(where[j] * 1024 + part * 512, 512)
                yield pltpu.make_async_copy(
                    source.at[pl.ds(row, 512), :],
                    held.at[j, t, pl.ds(i * 512, 512), :],
                    sem.at[j, t, i],
                )

    for j in range(n):
        for copy in copies(j):
            copy.start()
    for j in range(n):
        for copy in copies(j):
            copy.wait()
        at = 0
        for x in xs[j]:
            rows = slice(at, at + x.shape[0])
            at += x.shape[0]
            for t, (old, new) in enumerate(zip(before, sums)):
                term = jnp.dot(x[...], held[j, t], preferred_element_type=F32)
                if j > 0:
                    new[rows] += term
                elif first:
                    new[rows] = term
                else:
                    new[rows] = old[rows] + term
    if last:
        p = sum(
            lax.dot_general(
                y[...].astype(BF16), x[...], (((1,), (1,)), ((), ())), preferred_element_type=F32
            )
            for y, x in zip(sums, (x_mine, x_core))
        )
        row = documents(marked, column)
        tokens = column[pl.ds(pl.multiple_of(k * 256, 256), 256), :][:, :1]
        folded[...] = jnp.where(
            tokens == row[:, :256], p[:, :256], jnp.where(tokens == row[:, 256:], p[:, 256:], 0.0)
        )


def y_stage(xs, where, h, h_core, before, final=None):
    n = len(xs)
    first = before is None
    before = () if first else before
    xs = [x if isinstance(x, tuple) else (x,) for x in xs]
    parts = tuple(len(x) for x in xs)
    xs = [piece for x in xs for piece in x]
    last = final is not None
    if last:
        out_shape = [jax.ShapeDtypeStruct((256, 256), F32)]
        more = [pltpu.VMEM((256, 512), F32)] * 2 + [pltpu.VMEM((512, 128), F32)]
    else:
        out_shape = [jax.ShapeDtypeStruct((256, 512), F32)] * 2
        more = []
    final = final if last else ()
    return pl.pallas_call(
        functools.partial(y_body, parts, first, last),
        out_shape=out_shape,
        in_specs=[SMEM] + [VMEM] * len(xs) + [HBM, HBM] + [VMEM] * (len(before) + len(final)),
        out_specs=[VMEM] * len(out_shape),
        scratch_shapes=more
        + [pltpu.VMEM((n, 2, 1024, 512), BF16), pltpu.SemaphoreType.DMA((n, 2, 2))],
        compiler_params=pltpu.CompilerParams(vmem_limit_bytes=24 * MIB),
        cost_estimate=pl.CostEstimate(
            flops=n * (1 << 29), bytes_accessed=n * 2 * MIB + 2 * MIB, transcendentals=0
        ),
        name="y_stage",
    )(where, *xs, h, h_core, *before, *final)


def z_body(ks, core, *refs):
    parts, refs = refs[: len(ks)], refs[len(ks) :]
    n = sum(ks)
    mine, other, (out, column) = refs[:n], refs[n : 2 * n], refs[2 * n :]
    rows = pl.ds(pl.multiple_of(core[0] * 256, 256), 256)
    blocks = [part[i, ...] for part, count in zip(parts, ks) for i in range(count)]
    for i in range(n):
        row = documents(mine[i], column)
        low = jnp.where(column[rows, :][:, :1] == row[:, :256], blocks[i], jnp.zeros((), BF16))
        high = blocks[i] - low
        for t, d in enumerate((mine[i], other[i])):
            out[i, :, t * 512 : (t + 1) * 512] = (
                jnp.dot(low, d[:256], preferred_element_type=F32)
                + jnp.dot(high, d[256:512], preferred_element_type=F32)
            ).astype(BF16)


def z_stage(core, parts, mine, other):
    n = len(mine)
    return pl.pallas_call(
        functools.partial(z_body, tuple(part.shape[0] for part in parts)),
        out_shape=jax.ShapeDtypeStruct((n, 256, 1024), BF16),
        in_specs=[SMEM] + [VMEM] * (len(parts) + 2 * n),
        out_specs=VMEM,
        scratch_shapes=[pltpu.VMEM((512, 128), F32)],
        compiler_params=pltpu.CompilerParams(vmem_limit_bytes=24 * MIB),
        cost_estimate=pl.CostEstimate(
            flops=n * (1 << 28), bytes_accessed=n * 2 * MIB, transcendentals=0
        ),
        name="z_stage",
    )(core, *parts, *mine, *other)


def out_body(counts, sides, first, core, *refs):
    n = len(counts)
    rs = []
    for count in counts:
        rs.append(refs[:count])
        refs = refs[count:]
    near, far, refs = refs[0], refs[1], refs[2:]
    if not first:
        before, refs = refs[: len(sides)], refs[len(sides) :]
    outs, (held, z, sem) = refs[: len(sides)], refs[len(sides) :]
    k = core[0]
    width = 512 * len(sides)
    columns = pl.ds(sides[0] * 512, width)
    for i in range(n):
        at = i * 256
        for piece in rs[i]:
            rows = pl.ds(at, piece.shape[0])
            at += piece.shape[0]
            pltpu.make_async_copy(piece, held.at[rows], sem.at[i, 0]).start()
        place = core[1 + i]

        @pl.when(place < 2)
        def _():
            source = near.at[place, :, columns]
            pltpu.make_async_copy(source, z.at[pl.ds(i * 256, 256)], sem.at[i, 1]).start()

        @pl.when(place >= 2)
        def _():
            source = far.at[place - 2, :, columns]
            pltpu.make_async_copy(source, z.at[pl.ds(i * 256, 256)], sem.at[i, 1]).start()

    for i in range(n):
        rows = pl.ds(i * 256, 256)
        pltpu.make_async_copy(held.at[rows], held.at[rows], sem.at[i, 0]).wait()
        pltpu.make_async_copy(z.at[rows], z.at[rows], sem.at[i, 1]).wait()
    for i, part in enumerate((k, 1 - k)):
        rows = pl.ds(pl.multiple_of(part * 512, 512), 512)
        for t in range(len(sides)):
            term = lax.dot_general(
                held[:, i * 512 : (i + 1) * 512],
                z[:, t * 512 : (t + 1) * 512],
                (((0,), (0,)), ((), ())),
                preferred_element_type=F32,
            )
            outs[t][rows, :] = term if first else before[t][rows, :] + term


def out_stage(core, rs, near, far, sides, before):
    n = len(rs)
    counts = tuple(len(r) for r in rs)
    rs = [piece for r in rs for piece in r]
    return pl.pallas_call(
        functools.partial(out_body, counts, sides, not before),
        out_shape=[jax.ShapeDtypeStruct((1024, 512), F32)] * len(sides),
        in_specs=[SMEM] + [ANY] * (len(rs) + 2) + [VMEM] * len(before),
        out_specs=[VMEM] * len(sides),
        scratch_shapes=[
            pltpu.VMEM((n * 256, 1024), BF16),
            pltpu.VMEM((n * 256, 512 * len(sides)), BF16),
            pltpu.SemaphoreType.DMA((n, 2)),
        ],
        compiler_params=pltpu.CompilerParams(vmem_limit_bytes=24 * MIB),
        cost_estimate=pl.CostEstimate(
            flops=n * len(sides) * (1 << 28), bytes_accessed=n * MIB + 4 * MIB, transcendentals=0
        ),
        name="out_stage",
    )(core, *rs, near, far, *before)


EARLY = (0, 1, 2, 3, 4)


def step(inputs, grads, h_in, segments):
    yl, yh, z, k, x = (lax.axis_index(name) for name in AXES)
    core = jnp.stack([k])

    x_core = move(inputs, swap_core)
    x_rows = cut_rows(core, inputs, x_core)
    xs = gather(x_rows, z_up, z_down, z_far, swap_yh, 128)
    h_core = move(h_in, swap_core)
    h_in = pltpu.with_memory_space_constraint(h_in, pltpu.HBM)
    order = [(yh ^ a) * 4 + (z + b) % 4 for a in range(2) for b in range(4)]
    marked = jnp.concatenate([grads, jnp.broadcast_to(segments.astype(BF16), (16, 512))])

    sums = None
    for turn, chosen in enumerate(((0, 1, 3, 4), (2, 5, 7), (6,))):
        final = (inputs, x_core, marked) if turn == 2 else None
        where = jnp.stack([order[i] for i in chosen] + [k])
        sums = y_stage([xs[i] for i in chosen], where, h_in, h_core, sums, final)
    acc = sums[0]
    for where in (z_pair_a, z_pair_b, swap_yh):
        acc = acc + move(acc.astype(BF16), where).astype(F32)
    kh = acc.astype(BF16)
    pair = jnp.stack([kh, move(kh, swap_yl)])
    below = move(pair, x_up)
    above = move(pair, x_down)
    far = move(pair, x_far)

    ds = gather(marked, x_up, x_down, x_far, swap_yl, None)
    ds = [d[0] if isinstance(d, tuple) else d for d in ds]
    d_core = move(grads, swap_core)
    others = [d_core] + [move(ds[i], swap_core) for i in range(1, 8)]
    z_near = z_stage(core, (pair,), ds[::4], others[::4])
    chosen = (1, 5, 2, 6, 3, 7)
    z_rest = z_stage(
        core, (above, far, below), [ds[i] for i in chosen], [others[i] for i in chosen]
    )

    d_rows = cut_rows(core, grads, d_core)
    turned = move(move(d_rows, shear), reflect)
    rs = gather(turned, z_up, z_down, z_far, swap_yh, 128)
    rs = [r if isinstance(r, tuple) else (r,) for r in rs]
    places = [(z + i % 4 - 2 * x - 2 * k) % 4 * 2 + (yl ^ yh ^ (i // 4)) for i in range(8)]

    early, late = EARLY, [i for i in range(8) if i not in EARLY]
    pick = [jnp.stack([k] + [places[i] for i in some]) for some in (early, late)]
    blocks = [[rs[i] for i in some] for some in (early, late)]
    out_mine, out_send = out_stage(pick[0], blocks[0], z_near, z_rest, (0, 1), ())
    (out_send,) = out_stage(pick[1], blocks[1], z_near, z_rest, (1,), (out_send,))
    out_got = move(out_send, swap_core)
    (out_mine,) = out_stage(pick[1], blocks[1], z_near, z_rest, (0,), (out_mine,))
    return out_mine + out_got


def solution(mesh):
    fine = Mesh(mesh.devices.reshape(SIZES), AXES)
    col = ("yh", "z", "k")
    row = ("yl", "x")
    return jax.shard_map(
        step,
        mesh=fine,
        in_specs=(P(row, col), P(row, col), P(None, col), P(row, None)),
        out_specs=P(row, col),
        check_vma=False,
    )
```

```python
import functools

import jax
import jax.numpy as jnp
from jax import lax
from jax.experimental import pallas as pl
from jax.experimental.pallas import tpu as pltpu
from jax.sharding import Mesh, PartitionSpec as P


AXES = ("yl", "yh", "z", "k", "x")
SIZES = (2, 2, 4, 2, 4)

F32 = jnp.float32
BF16 = jnp.bfloat16


def linear(place):
    index = 0
    for part, size in zip(place, SIZES):
        index = index * size + part
    return index


def place_of(index):
    parts = []
    for size in reversed(SIZES):
        parts.append(index % size)
        index //= size
    return tuple(reversed(parts))


def move(value, where):
    pairs = [(i, linear(where(*place_of(i)))) for i in range(128)]
    return lax.ppermute(value, AXES, pairs)


def z_up(yl, yh, z, k, x):
    return yl, yh, (z + 1) % 4, k, x


def z_down(yl, yh, z, k, x):
    return yl, yh, (z - 1) % 4, k, x


def x_up(yl, yh, z, k, x):
    return yl, yh, z, k, (x + 1) % 4


def x_down(yl, yh, z, k, x):
    return yl, yh, z, k, (x - 1) % 4


def swap_yh(yl, yh, z, k, x):
    return yl, 1 - yh, z, k, x


def swap_yl(yl, yh, z, k, x):
    return 1 - yl, yh, z, k, x


def swap_core(yl, yh, z, k, x):
    return yl, yh, z, 1 - k, x


def z_pair_a(yl, yh, z, k, x):
    return yl, yh, z ^ 1, k, x


def z_pair_b(yl, yh, z, k, x):
    return yl, yh, (z + 1 if z % 2 else z - 1) % 4, k, x


def shear(yl, yh, z, k, x):
    return yl, yh, (z + x + 2 * k) % 4, k, x


def reflect(yl, yh, z, k, x):
    return yh, yl, z, k, (z - x - 2 * k) % 4


def z_far(yl, yh, z, k, x):
    return yl, yh, (z + 2) % 4, k, x


def x_far(yl, yh, z, k, x):
    return yl, yh, z, k, (x + 2) % 4


def gather(own, up, down, two, across, cut):
    below = move(own, up)
    above = move(own, down)
    over = move(own, across)
    over_below = move(over, up)
    over_above = move(over, down)
    if cut is None:
        far = (move(own, two),)
        over_far = (move(far[0], across),)
    else:
        far = (move(below[:cut], up), move(above[cut:], down))
        over_far = (move(far[0], across), move(far[1], across))
    return [own, above, far, below, over, over_above, over_far, over_below]


VMEM = pl.BlockSpec(memory_space=pltpu.VMEM)
HBM = pl.BlockSpec(memory_space=pltpu.HBM)
ANY = pl.BlockSpec(memory_space=pl.ANY)
SMEM = pl.BlockSpec(memory_space=pltpu.SMEM)
MIB = 1 << 20


def cut_body(core, mine, other, out):
    rows = pl.ds(pl.multiple_of(core[0] * 256, 256), 256)
    out[:, :512] = mine[rows, :]
    out[:, 512:] = other[rows, :]


def cut_rows(core, mine, other):
    return pl.pallas_call(
        cut_body,
        out_shape=jax.ShapeDtypeStruct((256, 1024), BF16),
        in_specs=[SMEM, VMEM, VMEM],
        out_specs=VMEM,
        compiler_params=pltpu.CompilerParams(vmem_limit_bytes=4 * MIB),
        cost_estimate=pl.CostEstimate(flops=0, bytes_accessed=MIB, transcendentals=0),
        name="cut_rows",
    )(core, mine, other)


def documents(marked, held):
    columns = jnp.transpose(marked[512:528, :].astype(F32))
    held[...] = jnp.broadcast_to(columns[:, :1], (512, 128))
    return marked[512:513, :].astype(F32)


def y_body(parts, first, last, where, *refs):
    n = len(parts)
    xs = []
    for count in parts:
        xs.append(refs[:count])
        refs = refs[count:]
    h, h_core, refs = refs[0], refs[1], refs[2:]
    if first:
        before = (None, None)
    else:
        before, refs = refs[:2], refs[2:]
    if last:
        x_mine, x_core, marked, folded, sum_mine, sum_core, column, held, sem = refs
        sums = (sum_mine, sum_core)
    else:
        sums, (held, sem) = refs[:2], refs[2:]
    k = where[n]

    def copies(j):
        for t, source in enumerate((h, h_core)):
            for i, part in enumerate((k, 1 - k)):
                row = pl.multiple_of(where[j] * 1024 + part * 512, 512)
                yield pltpu.make_async_copy(
                    source.at[pl.ds(row, 512), :],
                    held.at[j, t, pl.ds(i * 512, 512), :],
                    sem.at[j, t, i],
                )

    for j in range(n):
        for copy in copies(j):
            copy.start()
    for j in range(n):
        for copy in copies(j):
            copy.wait()
        at = 0
        for x in xs[j]:
            rows = slice(at, at + x.shape[0])
            at += x.shape[0]
            for t, (old, new) in enumerate(zip(before, sums)):
                term = jnp.dot(x[...], held[j, t], preferred_element_type=F32)
                if j > 0:
                    new[rows] += term
                elif first:
                    new[rows] = term
                else:
                    new[rows] = old[rows] + term
    if last:
        p = sum(
            lax.dot_general(
                y[...].astype(BF16), x[...], (((1,), (1,)), ((), ())), preferred_element_type=F32
            )
            for y, x in zip(sums, (x_mine, x_core))
        )
        row = documents(marked, column)
        tokens = column[pl.ds(pl.multiple_of(k * 256, 256), 256), :][:, :1]
        folded[...] = jnp.where(
            tokens == row[:, :256], p[:, :256], jnp.where(tokens == row[:, 256:], p[:, 256:], 0.0)
        )


def y_stage(xs, where, h, h_core, before, final=None):
    n = len(xs)
    first = before is None
    before = () if first else before
    xs = [x if isinstance(x, tuple) else (x,) for x in xs]
    parts = tuple(len(x) for x in xs)
    xs = [piece for x in xs for piece in x]
    last = final is not None
    if last:
        out_shape = [jax.ShapeDtypeStruct((256, 256), F32)]
        more = [pltpu.VMEM((256, 512), F32)] * 2 + [pltpu.VMEM((512, 128), F32)]
    else:
        out_shape = [jax.ShapeDtypeStruct((256, 512), F32)] * 2
        more = []
    final = final if last else ()
    return pl.pallas_call(
        functools.partial(y_body, parts, first, last),
        out_shape=out_shape,
        in_specs=[SMEM] + [VMEM] * len(xs) + [HBM, HBM] + [VMEM] * (len(before) + len(final)),
        out_specs=[VMEM] * len(out_shape),
        scratch_shapes=more
        + [pltpu.VMEM((n, 2, 1024, 512), BF16), pltpu.SemaphoreType.DMA((n, 2, 2))],
        compiler_params=pltpu.CompilerParams(vmem_limit_bytes=24 * MIB),
        cost_estimate=pl.CostEstimate(
            flops=n * (1 << 29), bytes_accessed=n * 2 * MIB + 2 * MIB, transcendentals=0
        ),
        name="y_stage",
    )(where, *xs, h, h_core, *before, *final)


def z_body(ks, core, *refs):
    parts, refs = refs[: len(ks)], refs[len(ks) :]
    n = sum(ks)
    mine, other, (out, column) = refs[:n], refs[n : 2 * n], refs[2 * n :]
    rows = pl.ds(pl.multiple_of(core[0] * 256, 256), 256)
    blocks = [part[i, ...] for part, count in zip(parts, ks) for i in range(count)]
    for i in range(n):
        row = documents(mine[i], column)
        low = jnp.where(column[rows, :][:, :1] == row[:, :256], blocks[i], jnp.zeros((), BF16))
        high = blocks[i] - low
        for t, d in enumerate((mine[i], other[i])):
            out[i, :, t * 512 : (t + 1) * 512] = (
                jnp.dot(low, d[:256], preferred_element_type=F32)
                + jnp.dot(high, d[256:512], preferred_element_type=F32)
            ).astype(BF16)


def z_stage(core, parts, mine, other):
    n = len(mine)
    return pl.pallas_call(
        functools.partial(z_body, tuple(part.shape[0] for part in parts)),
        out_shape=jax.ShapeDtypeStruct((n, 256, 1024), BF16),
        in_specs=[SMEM] + [VMEM] * (len(parts) + 2 * n),
        out_specs=VMEM,
        scratch_shapes=[pltpu.VMEM((512, 128), F32)],
        compiler_params=pltpu.CompilerParams(vmem_limit_bytes=24 * MIB),
        cost_estimate=pl.CostEstimate(
            flops=n * (1 << 28), bytes_accessed=n * 2 * MIB, transcendentals=0
        ),
        name="z_stage",
    )(core, *parts, *mine, *other)


def out_body(counts, sides, first, core, *refs):
    n = len(counts)
    rs = []
    for count in counts:
        rs.append(refs[:count])
        refs = refs[count:]
    near, far, refs = refs[0], refs[1], refs[2:]
    if not first:
        before, refs = refs[: len(sides)], refs[len(sides) :]
    outs, (held, z, sem) = refs[: len(sides)], refs[len(sides) :]
    k = core[0]
    width = 512 * len(sides)
    columns = pl.ds(sides[0] * 512, width)
    for i in range(n):
        at = i * 256
        for piece in rs[i]:
            rows = pl.ds(at, piece.shape[0])
            at += piece.shape[0]
            pltpu.make_async_copy(piece, held.at[rows], sem.at[i, 0]).start()
        place = core[1 + i]

        @pl.when(place < 2)
        def _():
            source = near.at[place, :, columns]
            pltpu.make_async_copy(source, z.at[pl.ds(i * 256, 256)], sem.at[i, 1]).start()

        @pl.when(place >= 2)
        def _():
            source = far.at[place - 2, :, columns]
            pltpu.make_async_copy(source, z.at[pl.ds(i * 256, 256)], sem.at[i, 1]).start()

    for i in range(n):
        rows = pl.ds(i * 256, 256)
        pltpu.make_async_copy(held.at[rows], held.at[rows], sem.at[i, 0]).wait()
        pltpu.make_async_copy(z.at[rows], z.at[rows], sem.at[i, 1]).wait()
    for i, part in enumerate((k, 1 - k)):
        rows = pl.ds(pl.multiple_of(part * 512, 512), 512)
        for t in range(len(sides)):
            term = lax.dot_general(
                held[:, i * 512 : (i + 1) * 512],
                z[:, t * 512 : (t + 1) * 512],
                (((0,), (0,)), ((), ())),
                preferred_element_type=F32,
            )
            total = term if first else before[t][rows, :] + term
            outs[t][rows, :] = total.astype(outs[t].dtype)


def out_stage(core, rs, near, far, sides, before, dtype=F32):
    n = len(rs)
    counts = tuple(len(r) for r in rs)
    rs = [piece for r in rs for piece in r]
    return pl.pallas_call(
        functools.partial(out_body, counts, sides, not before),
        out_shape=[jax.ShapeDtypeStruct((1024, 512), dtype)] * len(sides),
        in_specs=[SMEM] + [ANY] * (len(rs) + 2) + [VMEM] * len(before),
        out_specs=[VMEM] * len(sides),
        scratch_shapes=[
            pltpu.VMEM((n * 256, 1024), BF16),
            pltpu.VMEM((n * 256, 512 * len(sides)), BF16),
            pltpu.SemaphoreType.DMA((n, 2)),
        ],
        compiler_params=pltpu.CompilerParams(vmem_limit_bytes=24 * MIB),
        cost_estimate=pl.CostEstimate(
            flops=n * len(sides) * (1 << 28), bytes_accessed=n * MIB + 4 * MIB, transcendentals=0
        ),
        name="out_stage",
    )(core, *rs, near, far, *before)


EARLY = (0, 1, 3, 4)


def step(inputs, grads, h_in, segments):
    yl, yh, z, k, x = (lax.axis_index(name) for name in AXES)
    core = jnp.stack([k])

    x_core = move(inputs, swap_core)
    x_rows = cut_rows(core, inputs, x_core)
    xs = gather(x_rows, z_up, z_down, z_far, swap_yh, 128)
    h_core = move(h_in, swap_core)
    h_in = pltpu.with_memory_space_constraint(h_in, pltpu.HBM)
    order = [(yh ^ a) * 4 + (z + b) % 4 for a in range(2) for b in range(4)]
    marked = jnp.concatenate([grads, jnp.broadcast_to(segments.astype(BF16), (16, 512))])

    sums = None
    for turn, chosen in enumerate(((0, 1, 3, 4), (2, 5, 7), (6,))):
        final = (inputs, x_core, marked) if turn == 2 else None
        where = jnp.stack([order[i] for i in chosen] + [k])
        sums = y_stage([xs[i] for i in chosen], where, h_in, h_core, sums, final)
    acc = sums[0]
    for where in (z_pair_a, z_pair_b, swap_yh):
        acc = acc + move(acc.astype(BF16), where).astype(F32)
    kh = acc.astype(BF16)
    pair = jnp.stack([kh, move(kh, swap_yl)])
    below = move(pair, x_up)
    above = move(pair, x_down)
    far = move(pair, x_far)

    ds = gather(marked, x_up, x_down, x_far, swap_yl, None)
    ds = [d[0] if isinstance(d, tuple) else d for d in ds]
    d_core = move(grads, swap_core)
    others = [d_core] + [move(ds[i], swap_core) for i in range(1, 8)]
    z_near = z_stage(core, (pair,), ds[::4], others[::4])
    chosen = (1, 5, 2, 6, 3, 7)
    z_rest = z_stage(
        core, (above, far, below), [ds[i] for i in chosen], [others[i] for i in chosen]
    )

    d_rows = cut_rows(core, grads, d_core)
    turned = move(move(d_rows, shear), reflect)
    rs = gather(turned, z_up, z_down, z_far, swap_yh, 128)
    rs = [r if isinstance(r, tuple) else (r,) for r in rs]
    places = [(z + i % 4 - 2 * x - 2 * k) % 4 * 2 + (yl ^ yh ^ (i // 4)) for i in range(8)]

    early, late = EARLY, [i for i in range(8) if i not in EARLY]
    pick = [jnp.stack([k] + [places[i] for i in some]) for some in (early, late)]
    blocks = [[rs[i] for i in some] for some in (early, late)]
    out_mine, out_send = out_stage(pick[0], blocks[0], z_near, z_rest, (0, 1), ())
    (out_send,) = out_stage(pick[1], blocks[1], z_near, z_rest, (1,), (out_send,), BF16)
    out_got = move(out_send, swap_core)
    (out_mine,) = out_stage(pick[1], blocks[1], z_near, z_rest, (0,), (out_mine,))
    return out_mine + out_got.astype(F32)


def solution(mesh):
    fine = Mesh(mesh.devices.reshape(SIZES), AXES)
    col = ("yh", "z", "k")
    row = ("yl", "x")
    return jax.shard_map(
        step,
        mesh=fine,
        in_specs=(P(row, col), P(row, col), P(None, col), P(row, None)),
        out_specs=P(row, col),
        check_vma=False,
    )
```
